512 devices in a mesh: space: 64 (over y_hi, z, core), tm: 8 (over y_lo, x).
Axes of the slice: x: 4, y: 4 (y_hi: 2, y_lo: 2; y = y_hi * 2 + y_lo), z: 16, core: 2. Of those that a mesh axis runs over, the one named last changes fastest.
Arguments:
- row_orbitals: bfloat16 [32768, 2048], P('space', 'tm'), may hold values from -0.890625 to 0.890625
- column_orbitals: bfloat16 [1024, 2048], P('space', 'tm'), may hold values from -0.890625 to 0.890625
- occupation: int32 [2048], replicated, may hold values from 0 to 2
- order: int32 [2048], replicated, may hold values from 0 to 2047, each once
- levels: float32 [2048], replicated, may hold values from 0.1 to 1
- times: float32 [8], replicated, may hold values from 0.05 to 1.5
- quad_weights: float32 [8], replicated, may hold values from 0.5 to 1.5
- freqs: float32 [8], replicated, may hold values from 0.1 to 4
Outputs:
- spectrum: float32 [8, 32768, 1024], P(None, ('space', 'tm'))
The draws below stay inside these ranges and needn't reach their ends.
Inputs may be any that keep to these rules, and one draw needn't show every extreme that they name: `order`: each index of 0 to 2047 once.
All inputs are finite; a program needn't handle non-finite values.
Results may differ from the reference program's by a relative error of at most 0.0026.
Values may be sent and summed in bfloat16 or wider, within the bound.
A program may use at most 64 MiB of HBM per device.

```python
import math
import jax
import jax.numpy as jnp
from jax import lax

NORB = 2048
NFREQ = 8
NTIME = 8
NROW = 32768
NCOL = 1024


def set_ends(array, key, low, top_value):
    dims = array.shape
    place = [jax.random.randint(jax.random.fold_in(key, axis), (), 0, dims[axis]) for axis in range(len(dims))]
    array = array.at[tuple(place)].set(low)
    longest = dims.index(max(dims))
    place[longest] = (place[longest] + 1) % dims[longest]
    return array.at[tuple(place)].set(top_value)


def block_scale(own_key, dims, shards, low, largest):
    loudness, own = 1.0, jax.random.fold_in(own_key, 6)
    for axis_at, parts in shards:
        heights = jnp.exp(jax.random.uniform(jax.random.fold_in(own, axis_at), (parts,), jnp.float32, low / len(shards), largest / len(shards)))
        loudness = loudness * jnp.repeat(heights, dims[axis_at] // parts).reshape([-1 if axis == axis_at else 1 for axis in range(len(dims))])
    return loudness


def noise(stream_key, shape, deviation, bound, cuts=(), held_as=jnp.bfloat16):
    array = jax.random.normal(stream_key, shape, jnp.float32) * deviation
    if len(cuts) > 0:
        array = block_scale(stream_key, shape, cuts, -0.22, 0.18) * array
    return jnp.clip(array, min=-bound, max=bound).astype(held_as)


def setup_inputs(seed: int = 0) -> dict:
    seeds = jax.random.split(jax.random.key(seed), 9)
    return {
        "row_orbitals": noise(seeds[0], (NROW, NORB), (NORB ** -0.25), 0.890625, ((0, 64), (1, 8))),
        "column_orbitals": noise(seeds[1], (NCOL, NORB), (NORB ** -0.25), 0.890625, ((0, 64), (1, 8))),
        "occupation": set_ends(jax.random.randint(seeds[2], (NORB,), 0, 3), jax.random.fold_in(seeds[2], 1), 0, 2).astype(jnp.int32),
        "order": jax.random.permutation(seeds[3], NORB).astype(jnp.int32),
        "levels": jnp.clip(jnp.exp(jax.random.uniform(seeds[4], (NORB,), jnp.float32, math.log(0.1), math.log(1.0))), 0.1, 1.0),
        "times": jnp.clip(jnp.exp(jax.random.uniform(seeds[5], (NTIME,), jnp.float32, math.log(0.05), math.log(1.5))), 0.05, 1.5),
        "quad_weights": jnp.clip(jax.random.uniform(seeds[6], (NTIME,), jnp.float32, 0.5, 1.5), 0.5, 1.5),
        "freqs": jnp.clip(jnp.exp(jax.random.uniform(seeds[7], (NFREQ,), jnp.float32, math.log(0.1), math.log(4.0))), 0.1, 4.0),
    }


def reference(row_orbitals, column_orbitals, occupation, order, levels, times, quad_weights, freqs):
    energy = jnp.take(levels, order.astype(jnp.int32))
    filled = occupation.astype(jnp.float32) * 0.5
    cosines = quad_weights[None, :] * jnp.cos(freqs[:, None] * times[None, :])
    columns = column_orbitals.astype(jnp.float32)
    row_values = row_orbitals.astype(jnp.float32)
    spectrum = jnp.zeros((NFREQ, NROW, NCOL), jnp.float32)
    for which in range(NTIME):
        decays = jnp.exp(-times[which] * energy)
        scaled_full = lax.optimization_barrier((row_values * (filled * decays)[None, :]).astype(jnp.bfloat16)).astype(jnp.float32)
        scaled_empty = lax.optimization_barrier((row_values * ((1.0 - filled) * decays)[None, :]).astype(jnp.bfloat16)).astype(jnp.float32)
        green_full = jnp.dot(scaled_full, columns.T, precision=lax.Precision.HIGHEST)
        green_empty = jnp.dot(scaled_empty, columns.T, precision=lax.Precision.HIGHEST)
        polar = lax.optimization_barrier((green_full * green_empty).astype(jnp.bfloat16)).astype(jnp.float32)
        spectrum = spectrum + cosines[:, which][:, None, None] * polar[None]
    return spectrum
```

```python
import functools

import jax
import jax.numpy as jnp
from jax import lax
from jax.experimental import pallas as pl
from jax.experimental.pallas import tpu as pltpu
from jax.sharding import PartitionSpec as P

MESH = pl.DeviceIdType.MESH
NX, NY, NZ = 4, 4, 16


def here():
    space, tm = lax.axis_index("space"), lax.axis_index("tm")
    return tm % NX, (space // 32) * 2 + tm // NX, (space // 2) % NZ, space % 2


def device(x, y, z, core):
    return ((y // 2 * NZ + z) * 2 + core, (y % 2) * NX + x)


def position(rel):
    return 2 * rel - 1 if rel > 0 else -2 * rel


def gather_kernel(rows_hbm, columns_hbm, c_ref, r_ref, zs, zr, rs, rr, fs, fr, ss, sr, ks, kr, local):
    x, y, z, core = here()
    tm = lax.axis_index("tm")

    own = [
        pltpu.make_async_copy(columns_hbm.at[:, pl.ds(0, 128)], c_ref.at[core, 0, 0, x, y, 0], local.at[0]),
        pltpu.make_async_copy(columns_hbm.at[:, pl.ds(128, 128)], c_ref.at[core, 1, 0, y, x, 0], local.at[1]),
        pltpu.make_async_copy(rows_hbm.at[pl.ds(pl.multiple_of(tm * 64, 64), 64)], r_ref.at[tm], local.at[2]),
    ]
    for copy in own:
        copy.start()

    z_peers = [device(x, y, (z + d) % NZ, core) for d in (1, 15, 2, 14)]
    x_peers = [device((x + d) % NX, y, z, core) for d in (1, 3, 2)]
    y_peers = [device(x, (y + d) % NY, z, core) for d in (1, 3, 2)]
    y_twin = y // 2 * 2 + (1 - y % 2)
    row_peers = [device((x + dx) % NX, yy, z, core) for dx in range(NX) for yy in (y, y_twin) if dx or yy is y_twin]
    diagonal = [device((x + dx) % NX, y_twin, z, core) for dx in range(1, NX)]
    sibling = device(x, y, z, 1 - core)

    barrier = pltpu.get_barrier_semaphore()
    greeted = z_peers + x_peers + y_peers + diagonal + [sibling]
    for peer in greeted:
        pl.semaphore_signal(barrier, inc=1, device_id=peer, device_id_type=MESH)
    pl.semaphore_wait(barrier, len(greeted))

    started = []

    def send(src, dst, send_sem, recv_sem, peer):
        copy = pltpu.make_async_remote_copy(
            src_ref=src, dst_ref=dst, send_sem=send_sem, recv_sem=recv_sem, device_id=peer, device_id_type=MESH
        )
        copy.start()
        started.append(copy)
        return copy

    def spot(half, p):
        return c_ref.at[core, half, p // 4, (x, y)[half], (y, x)[half], p % 4]

    z_copies = {}

    def z_send(rel_from, rel_to):
        hop = rel_to - rel_from
        peer = device(x, y, (z - hop) % NZ, core)
        p = position(rel_to)
        z_copies[rel_to] = [
            send(spot(half, position(rel_from)), spot(half, p), zs.at[half, p], zr.at[half, p], peer) for half in (0, 1)
        ]

    def z_wait(*rels):
        for rel in rels:
            for copy in z_copies[rel]:
                copy.wait_recv()

    first_copies, second_copies, sib_copies = {}, {}, {}

    def first(g):
        first_copies[g] = []
        for i in range(3):
            for half, peers in ((0, y_peers), (1, x_peers)):
                ref = c_ref.at[core, half, g, (x, y)[half], (y, x)[half]]
                first_copies[g].append(send(ref, ref, fs.at[half, g, i], fr.at[half, g, i], peers[i]))

    def second(g):
        for copy in first_copies[g]:
            copy.wait_recv()
        second_copies[g] = []
        for i in range(3):
            for half, peers in ((0, x_peers), (1, y_peers)):
                ref = c_ref.at[core, half, g, (x, y)[half]]
                second_copies[g].append(send(ref, ref, ss.at[half, g, i], sr.at[half, g, i], peers[i]))

    def share(g):
        for copy in second_copies[g]:
            copy.wait_recv()
        sib_copies[g] = []
        for half in (0, 1):
            ref = c_ref.at[core, half, g]
            sib_copies[g].append(send(ref, ref, ks.at[half, g], kr.at[half, g], sibling))

    own[0].wait()
    own[1].wait()
    for rel in (2, -2, 1, -1):
        z_send(0, rel)

    row_copies = []
    for i, (dx, dy) in enumerate([(dx, dy) for dx in range(NX) for dy in (0, 1) if dx or dy]):
        px, py = (x + dx) % NX, (y_twin if dy else y)
        ptm = (py % 2) * NX + px
        src = rows_hbm.at[pl.ds(pl.multiple_of(ptm * 64, 64), 64)]
        row_copies.append(send(src, r_ref.at[tm], rs.at[i], rr.at[i], device(px, py, z, core)))

    z_wait(2)
    z_send(2, 4)
    z_send(2, 3)
    z_wait(-2)
    z_send(-2, -4)
    z_send(-2, -3)
    z_wait(1, -1)
    first(0)
    z_wait(4)
    z_send(4, 6)
    z_send(4, 5)
    z_wait(-4)
    z_send(-4, -6)
    z_send(-4, -5)
    z_wait(3, -3)
    first(1)
    second(0)
    z_wait(6)
    z_send(6, 8)
    z_send(6, 7)
    z_wait(-6)
    z_send(-6, -7)
    z_wait(5, -5)
    first(2)
    second(1)
    share(0)
    z_wait(8, 7, -7)
    first(3)
    second(2)
    share(1)
    second(3)
    share(2)
    share(3)
    own[2].wait()
    for copy in row_copies:
        copy.wait_recv()
    for g in range(4):
        for copy in sib_copies[g]:
            copy.wait_recv()
    for copy in started:
        copy.wait_send()


def compute_kernel(c_ref, r_ref, occ_ref, order_ref, levels_ref, times_ref, quad_ref, freqs_ref, o_ref, s_ref, w_ref, k_ref):
    step = pl.program_id(0)
    z = here()[2]

    @pl.when(step == 0)
    def _():
        order = order_ref[...]
        low, high = order % 128, order // 128
        n = order.shape[1]
        lanes = (lax.broadcasted_iota(jnp.int32, (128, n), 0) == low).astype(jnp.float32)
        picked = jnp.dot(
            levels_ref[...], lanes, precision=lax.Precision.HIGHEST, preferred_element_type=jnp.float32
        )
        mine = lax.broadcasted_iota(jnp.int32, picked.shape, 0) == high
        energy = jnp.sum(jnp.where(mine, picked, 0.0), axis=0, keepdims=True)
        filled = occ_ref[...].astype(jnp.float32) * 0.5
        for j in range(8):
            decay = jnp.exp(-times_ref[j] * energy)
            for which, share in ((0, filled), (1, 1.0 - filled)):
                weight = share * decay
                base = (which * 8 + j) * 64
                for t in range(8):
                    rows = r_ref[t].astype(jnp.float32)
                    s_ref[pl.ds(base, 64), pl.ds(t * 256, 256)] = (rows * weight[:, t * 256 : (t + 1) * 256]).astype(
                        jnp.bfloat16
                    )
        angle = jnp.zeros((8, 128), jnp.float32)
        row = lax.broadcasted_iota(jnp.int32, (8, 128), 0)
        lane = lax.broadcasted_iota(jnp.int32, (8, 128), 1)
        quad = jnp.zeros((8, 128), jnp.float32)
        for i in range(8):
            angle = jnp.where(row == i, freqs_ref[i], angle)
        times = jnp.zeros((8, 128), jnp.float32)
        for i in range(8):
            times = jnp.where(lane == i, times_ref[i], times)
            quad = jnp.where(lane == i, quad_ref[i], quad)
        cosines = quad * jnp.cos(angle * times)
        for k in range(8):
            for j in range(8):
                k_ref[k * 8 + j] = jnp.broadcast_to(cosines[k : k + 1, j : j + 1], (8, 128))

    y_hi, pair = step // 2, step % 2
    for i in range(8):
        rel = lax.rem(pair * 8 + i - z + 2 * NZ, NZ)
        pos = jnp.where(rel <= 8, jnp.maximum(2 * rel - 1, 0), 2 * (NZ - rel))
        g, slot = pos // 4, pos % 4
        for core in range(2):
            at = pl.ds(i * 32 + core * 16, 16)
            for t in range(8):
                y_lo, x = t // 4, t % 4
                y = y_hi * 2 + y_lo
                w_ref[at, pl.ds(t * 256, 128)] = c_ref[core, 0, g, x, y, slot]
                w_ref[at, pl.ds(t * 256 + 128, 128)] = c_ref[core, 1, g, y, x, slot]
    greens = lax.dot_general(
        s_ref[...], w_ref[...], (((1,), (1,)), ((), ())), preferred_element_type=jnp.float32
    )
    polar = (greens[:512] * greens[512:]).astype(jnp.bfloat16).astype(jnp.float32)
    for rt in range(8):
        for lt in range(2):
            parts = [polar[j * 64 + rt * 8 : j * 64 + rt * 8 + 8, lt * 128 : lt * 128 + 128] for j in range(8)]
            for k in range(8):
                total = k_ref[k * 8] * parts[0]
                for j in range(1, 8):
                    total = total + k_ref[k * 8 + j] * parts[j]
                o_ref[k, pl.ds(rt * 8, 8), pl.ds(lt * 128, 128)] = total


def body(row_orbitals, column_orbitals, occupation, order, levels, times, quad_weights, freqs):
    any_spec = pl.BlockSpec(memory_space=pl.ANY)
    vmem = pl.BlockSpec(memory_space=pltpu.VMEM)
    smem = pl.BlockSpec(memory_space=pltpu.SMEM)
    dma = pltpu.SemaphoreType.DMA
    columns, rows = pl.pallas_call(
        gather_kernel,
        out_shape=(
            pltpu.VMEM((2, 2, 4, 4, 4, 4, 16, 128), jnp.bfloat16),
            pltpu.VMEM((8, 64, 256), jnp.bfloat16),
        ),
        in_specs=[any_spec, any_spec],
        out_specs=(vmem, vmem),
        scratch_shapes=[
            dma((2, 16)), dma((2, 16)), dma((7,)), dma((7,)), dma((2, 4, 3)), dma((2, 4, 3)),
            dma((2, 4, 3)), dma((2, 4, 3)), dma((2, 4)), dma((2, 4)), dma((3,)),
        ],
        compiler_params=pltpu.CompilerParams(collective_id=0, has_side_effects=True, vmem_limit_bytes=16 * 2**20),
        name="gather",
    )(row_orbitals, column_orbitals)

    count = order.shape[0]
    return pl.pallas_call(
        compute_kernel,
        grid=(4,),
        out_shape=jax.ShapeDtypeStruct((8, 64, 1024), jnp.float32),
        in_specs=[vmem, vmem, vmem, vmem, vmem, smem, smem, smem],
        out_specs=pl.BlockSpec((8, 64, 256), lambda i: (0, 0, i)),
        scratch_shapes=[
            pltpu.VMEM((1024, 2048), jnp.bfloat16),
            pltpu.VMEM((256, 2048), jnp.bfloat16),
            pltpu.VMEM((64, 8, 128), jnp.float32),
        ],
        compiler_params=pltpu.CompilerParams(vmem_limit_bytes=40 * 2**20),
        name="compute",
    )(
        columns, rows, occupation.reshape(1, count), order.reshape(1, count), levels.reshape(count // 128, 128),
        times, quad_weights, freqs,
    )


def solution(mesh):
    placed = (P("space", "tm"), P("space", "tm"), P(), P(), P(), P(), P(), P())
    return jax.shard_map(
        body, mesh=mesh, in_specs=placed, out_specs=P(None, ("space", "tm"), None), check_vma=False
    )
```

```python
import functools

import jax
import jax.numpy as jnp
from jax import lax
from jax.experimental import pallas as pl
from jax.experimental.pallas import tpu as pltpu
from jax.sharding import PartitionSpec as P

MESH = pl.DeviceIdType.MESH
NX, NY, NZ = 4, 4, 16


def here():
    space, tm = lax.axis_index("space"), lax.axis_index("tm")
    y = lax.div(space, 32) * 2 + lax.div(tm, NX)
    return lax.rem(tm, NX), y, lax.rem(lax.div(space, 2), NZ), lax.rem(space, 2)


def device(x, y, z, core):
    return ((lax.div(y, 2) * NZ + z) * 2 + core, lax.rem(y, 2) * NX + x)


def position(rel):
    return 2 * rel - 1 if rel > 0 else -2 * rel


def gather_kernel(
    rows_hbm, columns_hbm, occ_hbm, order_hbm, levels_hbm, times_hbm, quad_hbm, freqs_hbm,
    c_ref, s_ref, k_ref,
    r_ref, occ_ref, order_ref, levels_ref, decay_ref, times_ref, quad_ref, freqs_ref,
    zs, zr, rs, rr, fs, fr, ss, sr, ks, kr, local,
):
    x, y, z, core = here()
    tm = lax.axis_index("tm")

    own = [
        pltpu.make_async_copy(src, dst, local.at[i])
        for i, (src, dst) in enumerate([
            (columns_hbm.at[:, pl.ds(0, 128)], c_ref.at[core, 0, 0, x, y, 0]),
            (columns_hbm.at[:, pl.ds(128, 128)], c_ref.at[core, 1, 0, y, x, 0]),
            (rows_hbm.at[pl.ds(pl.multiple_of(tm * 64, 64), 64)], r_ref.at[tm]),
            (occ_hbm, occ_ref),
            (order_hbm, order_ref),
            (levels_hbm, levels_ref),
            (times_hbm, times_ref),
            (quad_hbm, quad_ref),
            (freqs_hbm, freqs_ref),
        ])
    ]
    for copy in own:
        copy.start()

    z_peers = [device(x, y, lax.rem(z + d, NZ), core) for d in (4, 12, 3, 13, 2, 14, 1, 15)]
    x_peers = [device(lax.rem(x + d, NX), y, z, core) for d in (2, 1, 3)]
    y_peers = [device(x, lax.rem(y + d, NY), z, core) for d in (2, 1, 3)]
    y_twin = y + 1 - 2 * lax.rem(y, 2)
    diagonal = [device(lax.rem(x + dx, NX), y_twin, z, core) for dx in range(1, NX)]
    sibling = device(x, y, z, 1 - core)

    barrier = pltpu.get_barrier_semaphore()
    greeted = z_peers + x_peers + y_peers + diagonal + [sibling]
    for peer in greeted:
        pl.semaphore_signal(barrier, inc=1, device_id=peer, device_id_type=MESH)
    pl.semaphore_wait(barrier, len(greeted))

    started = []

    def send(src, dst, send_sem, recv_sem, peer):
        copy = pltpu.make_async_remote_copy(
            src_ref=src, dst_ref=dst, send_sem=send_sem, recv_sem=recv_sem, device_id=peer, device_id_type=MESH
        )
        copy.start()
        started.append(copy)
        return copy

    def spot(half, p):
        return c_ref.at[core, half, p // 4, (x, y)[half], (y, x)[half], p % 4]

    z_copies = {}

    def z_send(rel_from, rel_to):
        hop = rel_to - rel_from
        peer = device(x, y, lax.rem(z - hop + NZ, NZ), core)
        p = position(rel_to)
        z_copies[rel_to] = [
            send(spot(half, position(rel_from)), spot(half, p), zs.at[half, p], zr.at[half, p], peer) for half in (0, 1)
        ]

    def z_wait(*rels):
        for rel in rels:
            for copy in z_copies[rel]:
                copy.wait_recv()

    first_copies, second_copies, sib_copies = {}, {}, {}

    def first(g):
        first_copies[g] = []
        for i in range(3):
            for half, peers in ((0, y_peers), (1, x_peers)):
                ref = c_ref.at[core, half, g, (x, y)[half], (y, x)[half]]
                first_copies[g].append(send(ref, ref, fs.at[half, g, i], fr.at[half, g, i], peers[i]))

    def second(g):
        for copy in first_copies[g]:
            copy.wait_recv()
        second_copies[g] = []
        for i in range(3):
            for half, peers in ((0, x_peers), (1, y_peers)):
                ref = c_ref.at[core, half, g, (x, y)[half]]
                second_copies[g].append(send(ref, ref, ss.at[half, g, i], sr.at[half, g, i], peers[i]))

    def share(g):
        for copy in second_copies[g]:
            copy.wait_recv()
        sib_copies[g] = []
        for half in (0, 1):
            ref = c_ref.at[core, half, g]
            sib_copies[g].append(send(ref, ref, ks.at[half, g], kr.at[half, g], sibling))

    own[0].wait()
    own[1].wait()
    for rel in (4, -4, 2, -2, 1, -1, 3, -3):
        z_send(0, rel)

    row_copies = []
    for i, (dx, dy) in enumerate([(dx, dy) for dy in (1, 0) for dx in (2, 1, 3, 0) if dx or dy]):
        px, py = lax.rem(x + dx, NX), (y_twin if dy else y)
        ptm = lax.rem(py, 2) * NX + px
        src = rows_hbm.at[pl.ds(pl.multiple_of(ptm * 64, 64), 64)]
        row_copies.append(send(src, r_ref.at[tm], rs.at[i], rr.at[i], device(px, py, z, core)))

    for copy in own[2:]:
        copy.wait()
    order = order_ref[...]
    low, high = lax.rem(order, 128), lax.div(order, 128)
    n = order.shape[1]
    chosen = (lax.broadcasted_iota(jnp.int32, (128, n), 0) == low).astype(jnp.float32)
    picked = jnp.dot(levels_ref[...], chosen, precision=lax.Precision.HIGHEST, preferred_element_type=jnp.float32)
    mine = lax.broadcasted_iota(jnp.int32, picked.shape, 0) == high
    energy = jnp.sum(jnp.where(mine, picked, 0.0), axis=0, keepdims=True)
    row8 = lax.broadcasted_iota(jnp.int32, (8, n), 0)
    times8 = jnp.zeros((8, n), jnp.float32)
    for j in range(8):
        times8 = jnp.where(row8 == j, times_ref[j], times8)
    decays = jnp.exp(-times8 * energy)
    filled = occ_ref[...].astype(jnp.float32) * 0.5
    decay_ref[0] = filled * decays
    decay_ref[1] = (1.0 - filled) * decays

    row = lax.broadcasted_iota(jnp.int32, (8, 128), 0)
    lane = lax.broadcasted_iota(jnp.int32, (8, 128), 1)
    zero = jnp.zeros((8, 128), jnp.float32)
    freq, time, quad = zero, zero, zero
    for i in range(8):
        freq = jnp.where(row == i, freqs_ref[i], freq)
        time = jnp.where(lane == i, times_ref[i], time)
        quad = jnp.where(lane == i, quad_ref[i], quad)
    cosines = quad * jnp.cos(freq * time)
    for k in range(8):
        for j in range(8):
            k_ref[k * 8 + j] = jnp.broadcast_to(cosines[k : k + 1, j : j + 1], (8, 128))

    def scale(which):
        for t in range(8):
            rows = r_ref[t].astype(jnp.float32)
            for j in range(8):
                weight = decay_ref[which, j : j + 1, t * 256 : (t + 1) * 256]
                s_ref[pl.ds((which * 8 + j) * 64, 64), pl.ds(t * 256, 256)] = (rows * weight).astype(jnp.bfloat16)

    z_wait(1, -1, 2)
    first(0)
    z_wait(4, -4)
    for rel in (8, 6, 5, 7):
        z_send(4, rel)
        if rel < 8:
            z_send(-4, -rel)
    z_wait(-2, 3, -3)
    first(1)
    for copy in row_copies:
        copy.wait_recv()
    scale(0)
    second(0)
    z_wait(5, -5, 6)
    first(2)
    second(1)
    z_wait(-6, 7, -7, 8)
    first(3)
    share(0)
    scale(1)
    share(1)
    second(2)
    second(3)
    share(2)
    share(3)
    for g in range(4):
        for copy in sib_copies[g]:
            copy.wait_recv()
    for copy in started:
        copy.wait_send()


def compute_kernel(c_ref, s_ref, k_ref, o_ref, w_ref):
    step = pl.program_id(0)
    z = here()[2]
    y_hi, pair = lax.div(step, 2), lax.rem(step, 2)
    for i in range(8):
        rel = lax.rem(pair * 8 + i - z + 2 * NZ, NZ)
        pos = jnp.where(rel <= 8, jnp.maximum(2 * rel - 1, 0), 2 * (NZ - rel))
        g, slot = lax.div(pos, 4), lax.rem(pos, 4)
        for core in range(2):
            at = pl.ds(i * 32 + core * 16, 16)
            for t in range(8):
                y_lo, x = t // 4, t % 4
                y = y_hi * 2 + y_lo
                w_ref[at, pl.ds(t * 256, 128)] = c_ref[core, 0, g, x, y, slot]
                w_ref[at, pl.ds(t * 256 + 128, 128)] = c_ref[core, 1, g, y, x, slot]
    greens = lax.dot_general(
        s_ref[...], w_ref[...], (((1,), (1,)), ((), ())), preferred_element_type=jnp.float32
    )
    polar = (greens[:512] * greens[512:]).astype(jnp.bfloat16).astype(jnp.float32)
    for rt in range(8):
        for lt in range(2):
            parts = [polar[j * 64 + rt * 8 : j * 64 + rt * 8 + 8, lt * 128 : lt * 128 + 128] for j in range(8)]
            for k in range(8):
                total = k_ref[k * 8] * parts[0]
                for j in range(1, 8):
                    total = total + k_ref[k * 8 + j] * parts[j]
                o_ref[k, pl.ds(rt * 8, 8), pl.ds(lt * 128, 128)] = total


def body(row_orbitals, column_orbitals, occupation, order, levels, times, quad_weights, freqs):
    hbm = pl.BlockSpec(memory_space=pltpu.HBM)
    vmem = pl.BlockSpec(memory_space=pltpu.VMEM)
    dma = pltpu.SemaphoreType.DMA
    count = order.shape[0]
    columns, scaled, cosines = pl.pallas_call(
        gather_kernel,
        out_shape=(
            pltpu.VMEM((2, 2, 4, 4, 4, 4, 16, 128), jnp.bfloat16),
            pltpu.VMEM((1024, 2048), jnp.bfloat16),
            pltpu.VMEM((64, 8, 128), jnp.float32),
        ),
        in_specs=[hbm] * 8,
        out_specs=(vmem, vmem, vmem),
        scratch_shapes=[
            pltpu.VMEM((8, 64, 256), jnp.bfloat16),
            pltpu.VMEM((1, count), jnp.int32),
            pltpu.VMEM((1, count), jnp.int32),
            pltpu.VMEM((count // 128, 128), jnp.float32),
            pltpu.VMEM((2, 8, count), jnp.float32),
            pltpu.SMEM((8,), jnp.float32),
            pltpu.SMEM((8,), jnp.float32),
            pltpu.SMEM((8,), jnp.float32),
            dma((2, 16)), dma((2, 16)), dma((7,)), dma((7,)), dma((2, 4, 3)), dma((2, 4, 3)),
            dma((2, 4, 3)), dma((2, 4, 3)), dma((2, 4)), dma((2, 4)), dma((9,)),
        ],
        compiler_params=pltpu.CompilerParams(collective_id=0, has_side_effects=True, vmem_limit_bytes=58384384),
        name="gather",
    )(
        row_orbitals, column_orbitals, occupation.reshape(1, count), order.reshape(1, count),
        levels.reshape(count // 128, 128), times, quad_weights, freqs,
    )
    return pl.pallas_call(
        compute_kernel,
        grid=(4,),
        out_shape=jax.ShapeDtypeStruct((8, 64, 1024), jnp.float32),
        in_specs=[vmem, vmem, vmem],
        out_specs=pl.BlockSpec((8, 64, 256), lambda i: (0, 0, i)),
        scratch_shapes=[pltpu.VMEM((256, 2048), jnp.bfloat16)],
        compiler_params=pltpu.CompilerParams(vmem_limit_bytes=40 * 2**20),
        name="compute",
    )(columns, scaled, cosines)


def solution(mesh):
    placed = (P("space", "tm"), P("space", "tm"), P(), P(), P(), P(), P(), P())
    return jax.shard_map(
        body, mesh=mesh, in_specs=placed, out_specs=P(None, ("space", "tm"), None), check_vma=False
    )
```

```python
import functools

import jax
import jax.numpy as jnp
from jax import lax
from jax.experimental import pallas as pl
from jax.experimental.pallas import tpu as pltpu
from jax.sharding import PartitionSpec as P

MESH = pl.DeviceIdType.MESH
NX, NY, NZ = 4, 4, 16


def here():
    space, tm = lax.axis_index("space"), lax.axis_index("tm")
    y = lax.div(space, 32) * 2 + lax.div(tm, NX)
    return lax.rem(tm, NX), y, lax.rem(lax.div(space, 2), NZ), lax.rem(space, 2)


def device(x, y, z, core):
    return ((lax.div(y, 2) * NZ + z) * 2 + core, lax.rem(y, 2) * NX + x)


NEAR = {0: 0, 1: 1, -1: 2}
FAR = {
    2: (0, 0), -2: (0, 1), 3: (0, 2), -3: (0, 3), 4: (0, 4), -4: (0, 5),
    5: (1, 0), -5: (1, 1), 6: (1, 2), -6: (1, 3), 7: (1, 4), -7: (1, 5), 8: (1, 6),
}
WIDTH = (6, 7)
BASE = (48, 144)
HALF = 256


EARLY = (1, -1, 2, -2, 3, -3, 4, -4)
LATE = (5, -5, 6, -6, 7, -7, 8, 0)


def polar_of(planes, core, c_ref, s_ref, w_ref):
    for i, (y_hi, rel) in enumerate([(y_hi, rel) for y_hi in range(2) for rel in planes]):
        start, width = (NEAR[rel] * 16, 1) if rel in NEAR else (BASE[FAR[rel][0]] + FAR[rel][1], WIDTH[FAR[rel][0]])
        at = pl.ds(i * 16, 16)
        for t in range(8):
            x, y = t % 4, y_hi * 2 + t // 4
            w_ref[at, pl.ds(t * 256, 128)] = c_ref[core * 2 * HALF + start + (x * 4 + y) * width]
            w_ref[at, pl.ds(t * 256 + 128, 128)] = c_ref[(core * 2 + 1) * HALF + start + (y * 4 + x) * width]
    full, empty = (
        lax.dot_general(
            s_ref[pl.ds(which * 512, 512)], w_ref[...], (((1,), (1,)), ((), ())), preferred_element_type=jnp.float32
        )
        for which in range(2)
    )
    return (full * empty).astype(jnp.bfloat16)


def gather_kernel(
    rows_hbm, columns_hbm, occ_hbm, order_hbm, levels_hbm, times_hbm, quad_hbm, freqs_hbm,
    c_ref, s_ref, k_ref, p_ref, q_ref,
    w_ref, r_ref, occ_ref, order_ref, levels_ref, decay_ref, times_ref, quad_ref, freqs_ref,
    zs, zr, rs, rr, fs, fr, ss, sr, ps, pr, ks, kr, local,
):
    x, y, z, core = here()
    tm = lax.axis_index("tm")

    ab = (x * 4 + y, y * 4 + x)
    lead = (x, y)

    def tiles(half, start, count):
        return c_ref.at[pl.ds((core * 2 + half) * HALF + start, count)]

    def near(half, rel, first, count):
        return tiles(half, NEAR[rel] * 16 + first, count)

    def far(half, group, first, count):
        return tiles(half, BASE[group] + first * WIDTH[group], count * WIDTH[group])

    def far_one(half, rel):
        group, slot = FAR[rel]
        return tiles(half, BASE[group] + ab[half] * WIDTH[group] + slot, 1)

    own = [
        pltpu.make_async_copy(src, dst, local.at[i])
        for i, (src, dst) in enumerate([
            (columns_hbm.at[:, pl.ds(0, 128)], c_ref.at[core * 2 * HALF + ab[0]]),
            (columns_hbm.at[:, pl.ds(128, 128)], c_ref.at[(core * 2 + 1) * HALF + ab[1]]),
            (rows_hbm.at[pl.ds(pl.multiple_of(tm * 64, 64), 64)], r_ref.at[tm]),
            (occ_hbm, occ_ref),
            (order_hbm, order_ref),
            (levels_hbm, levels_ref),
            (times_hbm, times_ref),
            (quad_hbm, quad_ref),
            (freqs_hbm, freqs_ref),
        ])
    ]
    own[0].start()
    own[1].start()

    z_peers = [device(x, y, lax.rem(z + d, NZ), core) for d in (4, 12, 3, 13, 2, 14, 1, 15)]
    x_peers = [device(lax.rem(x + d, NX), y, z, core) for d in (2, 1, 3)]
    y_peers = [device(x, lax.rem(y + d, NY), z, core) for d in (2, 1, 3)]
    y_twin = y + 1 - 2 * lax.rem(y, 2)
    diagonal = [device(lax.rem(x + dx, NX), y_twin, z, core) for dx in range(1, NX)]
    sibling = device(x, y, z, 1 - core)

    barrier = pltpu.get_barrier_semaphore()
    greeted = z_peers + x_peers + y_peers + diagonal + [sibling]
    for peer in greeted:
        pl.semaphore_signal(barrier, inc=1, device_id=peer, device_id_type=MESH)
    for copy in own[2:]:
        copy.start()
    pl.semaphore_wait(barrier, len(greeted))

    started = []

    def send(src, dst, send_sem, recv_sem, peer):
        copy = pltpu.make_async_remote_copy(
            src_ref=src, dst_ref=dst, send_sem=send_sem, recv_sem=recv_sem, device_id=peer, device_id_type=MESH
        )
        copy.start()
        started.append(copy)
        return copy

    def wait(copies):
        for copy in copies:
            copy.wait_recv()

    z_copies = {}

    def z_send(rel_from, rel_to):
        peer = device(x, y, lax.rem(z - (rel_to - rel_from) + NZ, NZ), core)
        group, slot = FAR[rel_to]
        at = group * 6 + slot
        z_copies[rel_to] = [
            send(
                near(half, 0, ab[half], 1) if rel_from == 0 else far_one(half, rel_from),
                far_one(half, rel_to), zs.at[half, at], zr.at[half, at], peer,
            )
            for half in (0, 1)
        ]

    def spread(refs, peers, send_sems, recv_sems):
        return [
            send(refs[half], refs[half], send_sems.at[half, i], recv_sems.at[half, i], peers[half][i])
            for i in range(3)
            for half in (0, 1)
        ]

    def first(group):
        refs = [far(half, group, ab[half], 1) for half in (0, 1)]
        return spread(refs, (y_peers, x_peers), fs.at[group], fr.at[group])

    def second(group):
        refs = [far(half, group, lead[half] * 4, 4) for half in (0, 1)]
        return spread(refs, (x_peers, y_peers), ss.at[group], sr.at[group])

    def share(at, refs):
        return [send(refs[half], refs[half], ks.at[at, half], kr.at[at, half], sibling) for half in (0, 1)]

    own[0].wait()
    own[1].wait()
    for rel in (4, -4, 3, -3, 2, -2):
        z_send(0, rel)
    own_first = spread([near(half, 0, ab[half], 1) for half in (0, 1)], (y_peers, x_peers), fs.at[2], fr.at[2])

    row_copies = []
    for i, (dx, dy) in enumerate([(dx, dy) for dy in (1, 0) for dx in (2, 1, 3, 0) if dx or dy]):
        px, py = lax.rem(x + dx, NX), (y_twin if dy else y)
        ptm = lax.rem(py, 2) * NX + px
        src = rows_hbm.at[pl.ds(pl.multiple_of(ptm * 64, 64), 64)]
        row_copies.append(send(src, r_ref.at[tm], rs.at[i], rr.at[i], device(px, py, z, core)))

    for copy in own[2:]:
        copy.wait()
    order = order_ref[...]
    low, high = lax.rem(order, 128), lax.div(order, 128)
    n = order.shape[1]
    chosen = (lax.broadcasted_iota(jnp.int32, (128, n), 0) == low).astype(jnp.float32)
    picked = jnp.dot(levels_ref[...], chosen, precision=lax.Precision.HIGHEST, preferred_element_type=jnp.float32)
    mine = lax.broadcasted_iota(jnp.int32, picked.shape, 0) == high
    energy = jnp.sum(jnp.where(mine, picked, 0.0), axis=0, keepdims=True)
    row8 = lax.broadcasted_iota(jnp.int32, (8, n), 0)
    times8 = jnp.zeros((8, n), jnp.float32)
    for j in range(8):
        times8 = jnp.where(row8 == j, times_ref[j], times8)
    decays = jnp.exp(-times8 * energy)
    filled = occ_ref[...].astype(jnp.float32) * 0.5
    decay_ref[0] = filled * decays
    decay_ref[1] = (1.0 - filled) * decays

    row = lax.broadcasted_iota(jnp.int32, (8, 128), 0)
    lane = lax.broadcasted_iota(jnp.int32, (8, 128), 1)
    zero = jnp.zeros((8, 128), jnp.float32)
    freq, time, quad = zero, zero, zero
    for i in range(8):
        freq = jnp.where(row == i, freqs_ref[i], freq)
        time = jnp.where(lane == i, times_ref[i], time)
        quad = jnp.where(lane == i, quad_ref[i], quad)
    cosines = quad * jnp.cos(freq * time)
    for k in range(8):
        for j in range(8):
            k_ref[k * 8 + j] = jnp.broadcast_to(cosines[k : k + 1, j : j + 1], (8, 128))

    column = lax.broadcasted_iota(jnp.int32, (1, 512), 1)
    ahead = lax.rem(lax.div(column, 32) - z + NZ, NZ)
    place = jnp.where(ahead <= 8, jnp.maximum(2 * ahead - 1, 0), 2 * (NZ - ahead))
    rank, point = lax.rem(place + 15, 16), lax.rem(column, 32)
    other = jnp.where(lax.div(point, 16) == core, 0, 256)
    source = other + jnp.where(rank < 8, 0, 128) + lax.rem(rank, 8) * 16 + lax.rem(point, 16)
    chosen_rows = (lax.broadcasted_iota(jnp.int32, (512, 512), 0) == source).astype(jnp.float32).astype(jnp.bfloat16)
    q_ref[0] = chosen_rows[:, :256]
    q_ref[1] = chosen_rows[:, 256:]

    def scale(which):
        for t in range(8):
            rows = r_ref[t].astype(jnp.float32)
            for j in range(8):
                weight = decay_ref[which, j : j + 1, t * 256 : (t + 1) * 256]
                s_ref[pl.ds((which * 8 + j) * 64, 64), pl.ds(t * 256, 256)] = (rows * weight).astype(jnp.bfloat16)

    for rel in (4, -4):
        wait(z_copies[rel])
    for rel in (8, 6, 5, 7):
        z_send(4, rel)
        if rel < 8:
            z_send(-4, -rel)
    wait(own_first)
    own_second = spread([near(half, 0, lead[half] * 4, 4) for half in (0, 1)], (x_peers, y_peers), ss.at[2], sr.at[2])
    for rel in (2, -2, 3, -3):
        wait(z_copies[rel])
    first_a = first(0)
    wait(row_copies)
    scale(0)
    scale(1)
    wait(own_second)
    plane_copies = {}
    for i, rel in enumerate((1, -1)):
        peer = device(x, y, lax.rem(z - rel + NZ, NZ), core)
        plane_copies[rel] = [
            send(near(half, 0, 0, 16), near(half, rel, 0, 16), ps.at[i, half], pr.at[i, half], peer) for half in (0, 1)
        ]
    shared_own = share(0, [near(half, 0, 0, 16) for half in (0, 1)])
    for rel in (5, -5, 6, -6, 7, -7, 8):
        wait(z_copies[rel])
    first_b = first(1)
    wait(first_a)
    second_a = second(0)
    shared = []
    for i, rel in enumerate((1, -1)):
        wait(plane_copies[rel])
        shared += share(2 + i, [near(half, rel, 0, 16) for half in (0, 1)])
    wait(first_b)
    second_b = second(1)
    wait(second_a)
    shared += share(1, [far(half, 0, 0, 16) for half in (0, 1)])
    shared_b = share(4, [far(half, 1, lead[half] * 4, 4) for half in (0, 1)])
    p_ref[0] = polar_of(EARLY, core, c_ref, s_ref, w_ref.at[0])
    for at, (i, back) in enumerate(((1, 3), (2, 1), (0, 2))):
        wait(second_b[2 * i : 2 * i + 2])
        shared_b += share(5 + at, [far(half, 1, lax.rem(lead[half] + back, 4) * 4, 4) for half in (0, 1)])
    p_ref[1] = polar_of(LATE, core, c_ref, s_ref, w_ref.at[1])
    wait(shared)
    p_ref[2] = polar_of(EARLY, 1 - core, c_ref, s_ref, w_ref.at[0])
    wait(shared_own)
    wait(shared_b)
    for copy in started:
        copy.wait_send()


def compute_kernel(c_ref, s_ref, k_ref, p_ref, q_ref, o_hbm, w_ref, l_ref, o_ref, sem):
    last = polar_of(LATE, 1 - here()[3], c_ref, s_ref, w_ref)
    for y_hi in range(2):
        for group in range(3):
            l_ref[y_hi, :, pl.ds(group * 128, 128)] = p_ref[group, :, pl.ds(y_hi * 128, 128)]
        l_ref[y_hi, :, pl.ds(384, 128)] = last[:, y_hi * 128 : y_hi * 128 + 128]
    copies = []
    for step in range(4):
        y_hi, part = divmod(step, 2)
        polar = jnp.dot(l_ref[y_hi], q_ref[part], preferred_element_type=jnp.float32)
        for rt in range(8):
            for lt in range(2):
                parts = [polar[j * 64 + rt * 8 : j * 64 + rt * 8 + 8, lt * 128 : lt * 128 + 128] for j in range(8)]
                for k in range(8):
                    total = k_ref[k * 8] * parts[0]
                    for j in range(1, 8):
                        total = total + k_ref[k * 8 + j] * parts[j]
                    o_ref[step, k, pl.ds(rt * 8, 8), pl.ds(lt * 128, 128)] = total
        copy = pltpu.make_async_copy(o_ref.at[step], o_hbm.at[:, :, pl.ds(step * 256, 256)], sem.at[step])
        copy.start()
        copies.append(copy)
    for copy in copies:
        copy.wait()


def body(row_orbitals, column_orbitals, occupation, order, levels, times, quad_weights, freqs):
    hbm = pl.BlockSpec(memory_space=pltpu.HBM)
    vmem = pl.BlockSpec(memory_space=pltpu.VMEM)
    dma = pltpu.SemaphoreType.DMA
    count = order.shape[0]
    columns, scaled, cosines, polar, order_back = pl.pallas_call(
        gather_kernel,
        out_shape=(
            pltpu.VMEM((4 * HALF, 16, 128), jnp.bfloat16),
            pltpu.VMEM((1024, 2048), jnp.bfloat16),
            pltpu.VMEM((64, 8, 128), jnp.float32),
            pltpu.VMEM((3, 512, 256), jnp.bfloat16),
            pltpu.VMEM((2, 512, 256), jnp.bfloat16),
        ),
        in_specs=[hbm] * 8,
        out_specs=(vmem,) * 5,
        scratch_shapes=[
            pltpu.VMEM((2, 256, 2048), jnp.bfloat16),
            pltpu.VMEM((8, 64, 256), jnp.bfloat16),
            pltpu.VMEM((1, count), jnp.int32),
            pltpu.VMEM((1, count), jnp.int32),
            pltpu.VMEM((count // 128, 128), jnp.float32),
            pltpu.VMEM((2, 8, count), jnp.float32),
            pltpu.SMEM((8,), jnp.float32),
            pltpu.SMEM((8,), jnp.float32),
            pltpu.SMEM((8,), jnp.float32),
            dma((2, 13)), dma((2, 13)), dma((7,)), dma((7,)), dma((3, 2, 3)), dma((3, 2, 3)), dma((3, 2, 3)), dma((3, 2, 3)),
            dma((2, 2)), dma((2, 2)), dma((8, 2)), dma((8, 2)), dma((9,)),
        ],
        compiler_params=pltpu.CompilerParams(collective_id=0, has_side_effects=True, vmem_limit_bytes=67043328 - 9961472 - 8192),
        name="gather",
    )(
        row_orbitals, column_orbitals, occupation.reshape(1, count), order.reshape(1, count),
        levels.reshape(count // 128, 128), times, quad_weights, freqs,
    )
    return pl.pallas_call(
        compute_kernel,
        out_shape=jax.ShapeDtypeStruct((8, 64, 1024), jnp.float32),
        in_specs=[vmem] * 5,
        out_specs=hbm,
        scratch_shapes=[
            pltpu.VMEM((256, 2048), jnp.bfloat16),
            pltpu.VMEM((2, 512, 512), jnp.bfloat16),
            pltpu.VMEM((4, 8, 64, 256), jnp.float32),
            dma((4,)),
        ],
        compiler_params=pltpu.CompilerParams(vmem_limit_bytes=40 * 2**20),
        name="compute",
    )(columns, scaled, cosines, polar, order_back)


def solution(mesh):
    placed = (P("space", "tm"), P("space", "tm"), P(), P(), P(), P(), P(), P())
    return jax.shard_map(
        body, mesh=mesh, in_specs=placed, out_specs=P(None, ("space", "tm"), None), check_vma=False
    )
```

```python
import functools

import jax
import jax.numpy as jnp
from jax import lax
from jax.experimental import pallas as pl
from jax.experimental.pallas import tpu as pltpu
from jax.sharding import PartitionSpec as P

MESH = pl.DeviceIdType.MESH
NX, NY, NZ = 4, 4, 16


def here():
    space, tm = lax.axis_index("space"), lax.axis_index("tm")
    y = lax.div(space, 32) * 2 + lax.div(tm, NX)
    return lax.rem(tm, NX), y, lax.rem(lax.div(space, 2), NZ), lax.rem(space, 2)


def device(x, y, z, core):
    return ((lax.div(y, 2) * NZ + z) * 2 + core, lax.rem(y, 2) * NX + x)


NEAR = {0: 0, 1: 1, -1: 2, 2: 3, -2: 4}
FAR = {
    3: (0, 0), -3: (0, 1), 4: (0, 2), -4: (0, 3),
    5: (1, 0), -5: (1, 1), 6: (1, 2), -6: (1, 3), 7: (1, 4), -7: (1, 5), 8: (1, 6),
}
WIDTH = (4, 7)
BASE = (80, 144)
HALF = 256


EARLY = (1, -1, 2, -2, 3, -3, 4, -4)
LATE = (5, -5, 6, -6, 7, -7, 8, 0)


def polar_of(planes, core, c_ref, s_ref, w_ref):
    for i, (y_hi, rel) in enumerate([(y_hi, rel) for y_hi in range(2) for rel in planes]):
        start, width = (NEAR[rel] * 16, 1) if rel in NEAR else (BASE[FAR[rel][0]] + FAR[rel][1], WIDTH[FAR[rel][0]])
        at = pl.ds(i * 16, 16)
        for t in range(8):
            x, y = t % 4, y_hi * 2 + t // 4
            w_ref[at, pl.ds(t * 256, 128)] = c_ref[core * 2 * HALF + start + (x * 4 + y) * width]
            w_ref[at, pl.ds(t * 256 + 128, 128)] = c_ref[(core * 2 + 1) * HALF + start + (y * 4 + x) * width]
    full, empty = (
        lax.dot_general(
            s_ref[pl.ds(which * 512, 512)], w_ref[...], (((1,), (1,)), ((), ())), preferred_element_type=jnp.float32
        )
        for which in range(2)
    )
    return (full * empty).astype(jnp.bfloat16)


def gather_kernel(
    rows_hbm, columns_hbm, occ_hbm, order_hbm, levels_hbm, times_hbm, quad_hbm, freqs_hbm,
    c_ref, s_ref, k_ref, p_ref, q_ref,
    w_ref, r_ref, occ_ref, order_ref, levels_ref, decay_ref, times_ref, quad_ref, freqs_ref,
    zs, zr, rs, rr, fs, fr, ss, sr, ps, pr, ks, kr, local,
):
    x, y, z, core = here()
    tm = lax.axis_index("tm")

    ab = (x * 4 + y, y * 4 + x)
    lead = (x, y)

    def tiles(half, start, count):
        return c_ref.at[pl.ds((core * 2 + half) * HALF + start, count)]

    def near(half, rel, first, count):
        return tiles(half, NEAR[rel] * 16 + first, count)

    def far(half, group, first, count):
        return tiles(half, BASE[group] + first * WIDTH[group], count * WIDTH[group])

    def far_one(half, rel):
        group, slot = FAR[rel]
        return tiles(half, BASE[group] + ab[half] * WIDTH[group] + slot, 1)

    own = [
        pltpu.make_async_copy(src, dst, local.at[i])
        for i, (src, dst) in enumerate([
            (columns_hbm.at[:, pl.ds(0, 128)], c_ref.at[core * 2 * HALF + ab[0]]),
            (columns_hbm.at[:, pl.ds(128, 128)], c_ref.at[(core * 2 + 1) * HALF + ab[1]]),
            (rows_hbm.at[pl.ds(pl.multiple_of(tm * 64, 64), 64)], r_ref.at[tm]),
            (occ_hbm, occ_ref),
            (order_hbm, order_ref),
            (levels_hbm, levels_ref),
            (times_hbm, times_ref),
            (quad_hbm, quad_ref),
            (freqs_hbm, freqs_ref),
        ])
    ]
    own[0].start()
    own[1].start()

    z_peers = [device(x, y, lax.rem(z + d, NZ), core) for d in (4, 12, 3, 13, 2, 14, 1, 15)]
    x_peers = [device(lax.rem(x + d, NX), y, z, core) for d in (2, 1, 3)]
    y_peers = [device(x, lax.rem(y + d, NY), z, core) for d in (2, 1, 3)]
    y_twin = y + 1 - 2 * lax.rem(y, 2)
    diagonal = [device(lax.rem(x + dx, NX), y_twin, z, core) for dx in range(1, NX)]
    sibling = device(x, y, z, 1 - core)

    barrier = pltpu.get_barrier_semaphore()
    greeted = z_peers + x_peers + y_peers + diagonal + [sibling]
    for peer in greeted:
        pl.semaphore_signal(barrier, inc=1, device_id=peer, device_id_type=MESH)
    for copy in own[2:]:
        copy.start()
    pl.semaphore_wait(barrier, len(greeted))

    started = []

    def send(src, dst, send_sem, recv_sem, peer):
        copy = pltpu.make_async_remote_copy(
            src_ref=src, dst_ref=dst, send_sem=send_sem, recv_sem=recv_sem, device_id=peer, device_id_type=MESH
        )
        copy.start()
        started.append(copy)
        return copy

    def wait(copies):
        for copy in copies:
            copy.wait_recv()

    z_copies = {}

    def z_send(rel_from, rel_to):
        peer = device(x, y, lax.rem(z - (rel_to - rel_from) + NZ, NZ), core)
        group, slot = FAR[rel_to]
        at = group * 4 + slot
        z_copies[rel_to] = [
            send(
                near(half, 0, ab[half], 1) if rel_from == 0 else far_one(half, rel_from),
                far_one(half, rel_to), zs.at[half, at], zr.at[half, at], peer,
            )
            for half in (0, 1)
        ]

    def spread(refs, peers, send_sems, recv_sems):
        return [
            send(refs[half], refs[half], send_sems.at[half, i], recv_sems.at[half, i], peers[half][i])
            for i in range(3)
            for half in (0, 1)
        ]

    def first(group):
        refs = [far(half, group, ab[half], 1) for half in (0, 1)]
        return spread(refs, (y_peers, x_peers), fs.at[group], fr.at[group])

    def second(group):
        refs = [far(half, group, lead[half] * 4, 4) for half in (0, 1)]
        return spread(refs, (x_peers, y_peers), ss.at[group], sr.at[group])

    def share(at, refs):
        return [send(refs[half], refs[half], ks.at[at, half], kr.at[at, half], sibling) for half in (0, 1)]

    own[0].wait()
    own[1].wait()
    for rel in (4, -4, 3, -3):
        z_send(0, rel)
    own_first = spread([near(half, 0, ab[half], 1) for half in (0, 1)], (y_peers, x_peers), fs.at[2], fr.at[2])

    row_copies = []
    for i, (dx, dy) in enumerate([(dx, dy) for dy in (1, 0) for dx in (2, 1, 3, 0) if dx or dy]):
        px, py = lax.rem(x + dx, NX), (y_twin if dy else y)
        ptm = lax.rem(py, 2) * NX + px
        src = rows_hbm.at[pl.ds(pl.multiple_of(ptm * 64, 64), 64)]
        row_copies.append(send(src, r_ref.at[tm], rs.at[i], rr.at[i], device(px, py, z, core)))

    for copy in own[2:]:
        copy.wait()
    order = order_ref[...]
    low, high = lax.rem(order, 128), lax.div(order, 128)
    n = order.shape[1]
    chosen = (lax.broadcasted_iota(jnp.int32, (128, n), 0) == low).astype(jnp.float32)
    picked = jnp.dot(levels_ref[...], chosen, precision=lax.Precision.HIGHEST, preferred_element_type=jnp.float32)
    mine = lax.broadcasted_iota(jnp.int32, picked.shape, 0) == high
    energy = jnp.sum(jnp.where(mine, picked, 0.0), axis=0, keepdims=True)
    row8 = lax.broadcasted_iota(jnp.int32, (8, n), 0)
    times8 = jnp.zeros((8, n), jnp.float32)
    for j in range(8):
        times8 = jnp.where(row8 == j, times_ref[j], times8)
    decays = jnp.exp(-times8 * energy)
    filled = occ_ref[...].astype(jnp.float32) * 0.5
    decay_ref[0] = filled * decays
    decay_ref[1] = (1.0 - filled) * decays

    row = lax.broadcasted_iota(jnp.int32, (8, 128), 0)
    lane = lax.broadcasted_iota(jnp.int32, (8, 128), 1)
    zero = jnp.zeros((8, 128), jnp.float32)
    freq, time, quad = zero, zero, zero
    for i in range(8):
        freq = jnp.where(row == i, freqs_ref[i], freq)
        time = jnp.where(lane == i, times_ref[i], time)
        quad = jnp.where(lane == i, quad_ref[i], quad)
    cosines = quad * jnp.cos(freq * time)
    for k in range(8):
        for j in range(8):
            k_ref[k * 8 + j] = jnp.broadcast_to(cosines[k : k + 1, j : j + 1], (8, 128))

    column = lax.broadcasted_iota(jnp.int32, (1, 512), 1)
    ahead = lax.rem(lax.div(column, 32) - z + NZ, NZ)
    place = jnp.where(ahead <= 8, jnp.maximum(2 * ahead - 1, 0), 2 * (NZ - ahead))
    rank, point = lax.rem(place + 15, 16), lax.rem(column, 32)
    other = jnp.where(lax.div(point, 16) == core, 0, 256)
    source = other + jnp.where(rank < 8, 0, 128) + lax.rem(rank, 8) * 16 + lax.rem(point, 16)
    chosen_rows = (lax.broadcasted_iota(jnp.int32, (512, 512), 0) == source).astype(jnp.float32).astype(jnp.bfloat16)
    q_ref[0] = chosen_rows[:, :256]
    q_ref[1] = chosen_rows[:, 256:]

    def scale(which):
        for t in range(8):
            rows = r_ref[t].astype(jnp.float32)
            for j in range(8):
                weight = decay_ref[which, j : j + 1, t * 256 : (t + 1) * 256]
                s_ref[pl.ds((which * 8 + j) * 64, 64), pl.ds(t * 256, 256)] = (rows * weight).astype(jnp.bfloat16)

    for rel in (4, -4):
        wait(z_copies[rel])
    for rel in (8, 6, 5, 7):
        z_send(4, rel)
        if rel < 8:
            z_send(-4, -rel)
    wait(own_first)
    own_second = spread([near(half, 0, lead[half] * 4, 4) for half in (0, 1)], (x_peers, y_peers), ss.at[2], sr.at[2])
    for rel in (3, -3):
        wait(z_copies[rel])
    first_a = first(0)
    wait(row_copies)
    scale(0)
    scale(1)
    wait(own_second)
    plane_copies = {}
    for i, rel in enumerate((1, -1)):
        peer = device(x, y, lax.rem(z - rel + NZ, NZ), core)
        plane_copies[rel] = [
            send(near(half, 0, 0, 16), near(half, rel, 0, 16), ps.at[i, half], pr.at[i, half], peer) for half in (0, 1)
        ]
    shared_own = share(0, [near(half, 0, 0, 16) for half in (0, 1)])
    for rel in (5, -5, 6, -6, 7, -7, 8):
        wait(z_copies[rel])
    first_b = first(1)
    wait(first_a)
    second_a = second(0)
    shared = []
    for i, rel in enumerate((1, -1)):
        wait(plane_copies[rel])
        peer = device(x, y, lax.rem(z - rel + NZ, NZ), core)
        plane_copies[2 * rel] = [
            send(near(half, rel, 0, 16), near(half, 2 * rel, 0, 16), ps.at[2 + i, half], pr.at[2 + i, half], peer)
            for half in (0, 1)
        ]
        shared += share(2 + i, [near(half, rel, 0, 16) for half in (0, 1)])
    wait(first_b)
    second_b = second(1)
    wait(second_a)
    shared += share(1, [far(half, 0, 0, 16) for half in (0, 1)])
    shared_b = share(6, [far(half, 1, lead[half] * 4, 4) for half in (0, 1)])
    for i, rel in enumerate((2, -2)):
        wait(plane_copies[rel])
        shared += share(4 + i, [near(half, rel, 0, 16) for half in (0, 1)])
    p_ref[0] = polar_of(EARLY, core, c_ref, s_ref, w_ref.at[0])
    for at, (i, back) in enumerate(((1, 3), (2, 1), (0, 2))):
        wait(second_b[2 * i : 2 * i + 2])
        shared_b += share(7 + at, [far(half, 1, lax.rem(lead[half] + back, 4) * 4, 4) for half in (0, 1)])
    p_ref[1] = polar_of(LATE, core, c_ref, s_ref, w_ref.at[1])
    wait(shared)
    p_ref[2] = polar_of(EARLY, 1 - core, c_ref, s_ref, w_ref.at[0])
    wait(shared_own)
    wait(shared_b)
    for copy in started:
        copy.wait_send()


def compute_kernel(c_ref, s_ref, k_ref, p_ref, q_ref, o_hbm, w_ref, l_ref, o_ref, sem):
    last = polar_of(LATE, 1 - here()[3], c_ref, s_ref, w_ref)
    for y_hi in range(2):
        for group in range(3):
            l_ref[y_hi, :, pl.ds(group * 128, 128)] = p_ref[group, :, pl.ds(y_hi * 128, 128)]
        l_ref[y_hi, :, pl.ds(384, 128)] = last[:, y_hi * 128 : y_hi * 128 + 128]
    copies = []
    for step in range(4):
        y_hi, part = divmod(step, 2)
        polar = [
            jnp.dot(l_ref[y_hi, pl.ds(h * 256, 256)], q_ref[part], preferred_element_type=jnp.float32) for h in range(2)
        ]
        for rt in range(8):
            for lt in range(2):
                parts = [
                    polar[j // 4][j % 4 * 64 + rt * 8 : j % 4 * 64 + rt * 8 + 8, lt * 128 : lt * 128 + 128] for j in range(8)
                ]
                for k in range(8):
                    total = k_ref[k * 8] * parts[0]
                    for j in range(1, 8):
                        total = total + k_ref[k * 8 + j] * parts[j]
                    o_ref[step, k, pl.ds(rt * 8, 8), pl.ds(lt * 128, 128)] = total
        copy = pltpu.make_async_copy(o_ref.at[step], o_hbm.at[:, :, pl.ds(step * 256, 256)], sem.at[step])
        copy.start()
        copies.append(copy)
    for copy in copies:
        copy.wait()


def body(row_orbitals, column_orbitals, occupation, order, levels, times, quad_weights, freqs):
    hbm = pl.BlockSpec(memory_space=pltpu.HBM)
    vmem = pl.BlockSpec(memory_space=pltpu.VMEM)
    dma = pltpu.SemaphoreType.DMA
    count = order.shape[0]
    columns, scaled, cosines, polar, order_back = pl.pallas_call(
        gather_kernel,
        out_shape=(
            pltpu.VMEM((4 * HALF, 16, 128), jnp.bfloat16),
            pltpu.VMEM((1024, 2048), jnp.bfloat16),
            pltpu.VMEM((64, 8, 128), jnp.float32),
            pltpu.VMEM((3, 512, 256), jnp.bfloat16),
            pltpu.VMEM((2, 512, 256), jnp.bfloat16),
        ),
        in_specs=[hbm] * 8,
        out_specs=(vmem,) * 5,
        scratch_shapes=[
            pltpu.VMEM((2, 256, 2048), jnp.bfloat16),
            pltpu.VMEM((8, 64, 256), jnp.bfloat16),
            pltpu.VMEM((1, count), jnp.int32),
            pltpu.VMEM((1, count), jnp.int32),
            pltpu.VMEM((count // 128, 128), jnp.float32),
            pltpu.VMEM((2, 8, count), jnp.float32),
            pltpu.SMEM((8,), jnp.float32),
            pltpu.SMEM((8,), jnp.float32),
            pltpu.SMEM((8,), jnp.float32),
            dma((2, 11)), dma((2, 11)), dma((7,)), dma((7,)), dma((3, 2, 3)), dma((3, 2, 3)), dma((3, 2, 3)), dma((3, 2, 3)),
            dma((4, 2)), dma((4, 2)), dma((10, 2)), dma((10, 2)), dma((9,)),
        ],
        compiler_params=pltpu.CompilerParams(collective_id=0, has_side_effects=True, vmem_limit_bytes=67043328 - 9961472 - 8192),
        name="gather",
    )(
        row_orbitals, column_orbitals, occupation.reshape(1, count), order.reshape(1, count),
        levels.reshape(count // 128, 128), times, quad_weights, freqs,
    )
    return pl.pallas_call(
        compute_kernel,
        out_shape=jax.ShapeDtypeStruct((8, 64, 1024), jnp.float32),
        in_specs=[vmem] * 5,
        out_specs=hbm,
        scratch_shapes=[
            pltpu.VMEM((256, 2048), jnp.bfloat16),
            pltpu.VMEM((2, 512, 512), jnp.bfloat16),
            pltpu.VMEM((4, 8, 64, 256), jnp.float32),
            dma((4,)),
        ],
        compiler_params=pltpu.CompilerParams(vmem_limit_bytes=40 * 2**20),
        name="compute",
    )(columns, scaled, cosines, polar, order_back)


def solution(mesh):
    placed = (P("space", "tm"), P("space", "tm"), P(), P(), P(), P(), P(), P())
    return jax.shard_map(
        body, mesh=mesh, in_specs=placed, out_specs=P(None, ("space", "tm"), None), check_vma=False
    )
```

```python
import functools

import jax
import jax.numpy as jnp
from jax import lax
from jax.experimental import pallas as pl
from jax.experimental.pallas import tpu as pltpu
from jax.sharding import PartitionSpec as P

MESH = pl.DeviceIdType.MESH
NX, NY, NZ = 4, 4, 16


def here():
    space, tm = lax.axis_index("space"), lax.axis_index("tm")
    y = lax.div(space, 32) * 2 + lax.div(tm, NX)
    return lax.rem(tm, NX), y, lax.rem(lax.div(space, 2), NZ), lax.rem(space, 2)


def device(x, y, z, core):
    return ((lax.div(y, 2) * NZ + z) * 2 + core, lax.rem(y, 2) * NX + x)


NEAR = {0: 0, 1: 1, -1: 2, 2: 3, -2: 4}
FAR = {
    3: (0, 0), -3: (0, 1), 4: (0, 2), -4: (0, 3),
    5: (1, 0), -5: (1, 1), 6: (1, 2), -6: (1, 3), 7: (1, 4), -7: (1, 5), 8: (1, 6),
}
WIDTH = (4, 7)
BASE = (80, 144)
HALF = 256


EARLY = (1, -1, 2, -2, 3, -3, 4, -4)
LATE = (5, -5, 6, -6, 7, -7, 8, 0)


def polar_of(planes, core, c_ref, s_ref, w_ref):
    for i, (y_hi, rel) in enumerate([(y_hi, rel) for y_hi in range(2) for rel in planes]):
        start, width = (NEAR[rel] * 16, 1) if rel in NEAR else (BASE[FAR[rel][0]] + FAR[rel][1], WIDTH[FAR[rel][0]])
        at = pl.ds(i * 16, 16)
        for t in range(8):
            x, y = t % 4, y_hi * 2 + t // 4
            w_ref[at, pl.ds(t * 256, 128)] = c_ref[core * 2 * HALF + start + (x * 4 + y) * width]
            w_ref[at, pl.ds(t * 256 + 128, 128)] = c_ref[(core * 2 + 1) * HALF + start + (y * 4 + x) * width]
    full, empty = (
        lax.dot_general(
            s_ref[pl.ds(which * 512, 512)], w_ref[...], (((1,), (1,)), ((), ())), preferred_element_type=jnp.float32
        )
        for which in range(2)
    )
    return (full * empty).astype(jnp.bfloat16)


def gather_kernel(
    rows_hbm, columns_hbm, occ_hbm, order_hbm, levels_hbm, times_hbm, quad_hbm, freqs_hbm,
    c_ref, s_ref, k_ref, p_ref, q_ref,
    w_ref, r_ref, occ_ref, order_ref, levels_ref, decay_ref, times_ref, quad_ref, freqs_ref,
    zs, zr, rs, rr, fs, fr, ss, sr, ps, pr, ks, kr, local,
):
    x, y, z, core = here()
    tm = lax.axis_index("tm")

    ab = (x * 4 + y, y * 4 + x)
    lead = (x, y)

    def tiles(half, start, count):
        return c_ref.at[pl.ds((core * 2 + half) * HALF + start, count)]

    def near(half, rel, first, count):
        return tiles(half, NEAR[rel] * 16 + first, count)

    def far(half, group, first, count):
        return tiles(half, BASE[group] + first * WIDTH[group], count * WIDTH[group])

    def far_one(half, rel):
        group, slot = FAR[rel]
        return tiles(half, BASE[group] + ab[half] * WIDTH[group] + slot, 1)

    own = [
        pltpu.make_async_copy(src, dst, local.at[i])
        for i, (src, dst) in enumerate([
            (columns_hbm.at[:, pl.ds(0, 128)], c_ref.at[core * 2 * HALF + ab[0]]),
            (columns_hbm.at[:, pl.ds(128, 128)], c_ref.at[(core * 2 + 1) * HALF + ab[1]]),
            (rows_hbm.at[pl.ds(pl.multiple_of(tm * 64, 64), 64)], r_ref.at[tm]),
            (occ_hbm, occ_ref),
            (order_hbm, order_ref),
            (levels_hbm, levels_ref),
            (times_hbm, times_ref),
            (quad_hbm, quad_ref),
            (freqs_hbm, freqs_ref),
        ])
    ]
    own[0].start()
    own[1].start()

    z_peers = [device(x, y, lax.rem(z + d, NZ), core) for d in (4, 12, 3, 13, 2, 14, 1, 15)]
    x_peers = [device(lax.rem(x + d, NX), y, z, core) for d in (2, 1, 3)]
    y_peers = [device(x, lax.rem(y + d, NY), z, core) for d in (2, 1, 3)]
    y_twin = y + 1 - 2 * lax.rem(y, 2)
    diagonal = [device(lax.rem(x + dx, NX), y_twin, z, core) for dx in range(1, NX)]
    sibling = device(x, y, z, 1 - core)

    barrier = pltpu.get_barrier_semaphore()
    greeted = z_peers + x_peers + y_peers + diagonal + [sibling]
    for peer in greeted:
        pl.semaphore_signal(barrier, inc=1, device_id=peer, device_id_type=MESH)
    for copy in own[2:]:
        copy.start()
    pl.semaphore_wait(barrier, len(greeted))

    started = []

    def send(src, dst, send_sem, recv_sem, peer):
        copy = pltpu.make_async_remote_copy(
            src_ref=src, dst_ref=dst, send_sem=send_sem, recv_sem=recv_sem, device_id=peer, device_id_type=MESH
        )
        copy.start()
        started.append(copy)
        return copy

    def wait(copies):
        for copy in copies:
            copy.wait_recv()

    z_copies = {}

    def z_send(rel_from, rel_to):
        peer = device(x, y, lax.rem(z - (rel_to - rel_from) + NZ, NZ), core)
        group, slot = FAR[rel_to]
        at = group * 4 + slot
        z_copies[rel_to] = [
            send(
                near(half, 0, ab[half], 1) if rel_from == 0 else far_one(half, rel_from),
                far_one(half, rel_to), zs.at[half, at], zr.at[half, at], peer,
            )
            for half in (0, 1)
        ]

    def spread(refs, peers, send_sems, recv_sems):
        return [
            send(refs[half], refs[half], send_sems.at[half, i], recv_sems.at[half, i], peers[half][i])
            for i in range(3)
            for half in (0, 1)
        ]

    def first(group):
        refs = [far(half, group, ab[half], 1) for half in (0, 1)]
        return spread(refs, (y_peers, x_peers), fs.at[group], fr.at[group])

    def second(group):
        refs = [far(half, group, lead[half] * 4, 4) for half in (0, 1)]
        return spread(refs, (x_peers, y_peers), ss.at[group], sr.at[group])

    def share(at, refs):
        return [send(refs[half], refs[half], ks.at[at, half], kr.at[at, half], sibling) for half in (0, 1)]

    own[0].wait()
    own[1].wait()
    for rel in (4, -4, 3, -3):
        z_send(0, rel)
    own_first = spread([near(half, 0, ab[half], 1) for half in (0, 1)], (y_peers, x_peers), fs.at[2], fr.at[2])

    row_copies = []
    for i, (dx, dy) in enumerate([(dx, dy) for dy in (1, 0) for dx in (2, 1, 3, 0) if dx or dy]):
        px, py = lax.rem(x + dx, NX), (y_twin if dy else y)
        ptm = lax.rem(py, 2) * NX + px
        src = rows_hbm.at[pl.ds(pl.multiple_of(ptm * 64, 64), 64)]
        row_copies.append(send(src, r_ref.at[tm], rs.at[i], rr.at[i], device(px, py, z, core)))

    for copy in own[2:]:
        copy.wait()
    order = order_ref[...]
    low, high = lax.rem(order, 128), lax.div(order, 128)
    n = order.shape[1]
    chosen = (lax.broadcasted_iota(jnp.int32, (128, n), 0) == low).astype(jnp.float32)
    picked = jnp.dot(levels_ref[...], chosen, precision=lax.Precision.HIGHEST, preferred_element_type=jnp.float32)
    mine = lax.broadcasted_iota(jnp.int32, picked.shape, 0) == high
    energy = jnp.sum(jnp.where(mine, picked, 0.0), axis=0, keepdims=True)
    row8 = lax.broadcasted_iota(jnp.int32, (8, n), 0)
    times8 = jnp.zeros((8, n), jnp.float32)
    for j in range(8):
        times8 = jnp.where(row8 == j, times_ref[j], times8)
    decays = jnp.exp(-times8 * energy)
    filled = occ_ref[...].astype(jnp.float32) * 0.5
    decay_ref[0] = filled * decays
    decay_ref[1] = (1.0 - filled) * decays

    row = lax.broadcasted_iota(jnp.int32, (8, 128), 0)
    lane = lax.broadcasted_iota(jnp.int32, (8, 128), 1)
    zero = jnp.zeros((8, 128), jnp.float32)
    freq, time, quad = zero, zero, zero
    for i in range(8):
        freq = jnp.where(row == i, freqs_ref[i], freq)
        time = jnp.where(lane == i, times_ref[i], time)
        quad = jnp.where(lane == i, quad_ref[i], quad)
    cosines = quad * jnp.cos(freq * time)
    for k in range(8):
        for j in range(8):
            k_ref[k * 8 + j] = jnp.broadcast_to(cosines[k : k + 1, j : j + 1], (8, 128))

    column = lax.broadcasted_iota(jnp.int32, (1, 512), 1)
    ahead = lax.rem(lax.div(column, 32) - z + NZ, NZ)
    place = jnp.where(ahead <= 8, jnp.maximum(2 * ahead - 1, 0), 2 * (NZ - ahead))
    rank, point = lax.rem(place + 15, 16), lax.rem(column, 32)
    other = jnp.where(lax.div(point, 16) == core, 0, 256)
    source = other + jnp.where(rank < 8, 0, 128) + lax.rem(rank, 8) * 16 + lax.rem(point, 16)
    chosen_rows = (lax.broadcasted_iota(jnp.int32, (512, 512), 0) == source).astype(jnp.float32).astype(jnp.bfloat16)
    q_ref[0] = chosen_rows[:, :256]
    q_ref[1] = chosen_rows[:, 256:]

    def scale(which):
        for t in range(8):
            rows = r_ref[t].astype(jnp.float32)
            for j in range(8):
                weight = decay_ref[which, j : j + 1, t * 256 : (t + 1) * 256]
                s_ref[pl.ds((which * 8 + j) * 64, 64), pl.ds(t * 256, 256)] = (rows * weight).astype(jnp.bfloat16)

    for rel in (4, -4):
        wait(z_copies[rel])
    for rel in (8, 6, 5, 7):
        z_send(4, rel)
        if rel < 8:
            z_send(-4, -rel)
    wait(own_first)
    own_second = spread([near(half, 0, lead[half] * 4, 4) for half in (0, 1)], (x_peers, y_peers), ss.at[2], sr.at[2])
    for rel in (3, -3):
        wait(z_copies[rel])
    first_a = first(0)
    wait(row_copies)
    scale(0)
    scale(1)
    wait(own_second)
    plane_copies = {}
    for i, rel in enumerate((1, -1)):
        peer = device(x, y, lax.rem(z - rel + NZ, NZ), core)
        plane_copies[rel] = [
            send(near(half, 0, 0, 16), near(half, rel, 0, 16), ps.at[i, half], pr.at[i, half], peer) for half in (0, 1)
        ]
    shared_own = share(0, [near(half, 0, 0, 16) for half in (0, 1)])
    for rel in (5, -5, 6, -6, 7, -7, 8):
        wait(z_copies[rel])
    first_b = first(1)
    wait(first_a)
    second_a = second(0)
    shared = []
    for i, rel in enumerate((1, -1)):
        wait(plane_copies[rel])
        peer = device(x, y, lax.rem(z - rel + NZ, NZ), core)
        plane_copies[2 * rel] = [
            send(near(half, rel, 0, 16), near(half, 2 * rel, 0, 16), ps.at[2 + i, half], pr.at[2 + i, half], peer)
            for half in (0, 1)
        ]
        shared += share(2 + i, [near(half, rel, 0, 16) for half in (0, 1)])
    wait(first_b)
    second_b = second(1)
    shared_b = share(6, [far(half, 1, lead[half] * 4, 4) for half in (0, 1)])
    wait(second_a)
    shared += share(1, [far(half, 0, 0, 16) for half in (0, 1)])
    for i, rel in enumerate((2, -2)):
        wait(plane_copies[rel])
        shared += share(4 + i, [near(half, rel, 0, 16) for half in (0, 1)])
    p_ref[0] = polar_of(EARLY, core, c_ref, s_ref, w_ref.at[0])
    for at, (i, back) in enumerate(((1, 3), (2, 1), (0, 2))):
        wait(second_b[2 * i : 2 * i + 2])
        shared_b += share(7 + at, [far(half, 1, lax.rem(lead[half] + back, 4) * 4, 4) for half in (0, 1)])
    p_ref[1] = polar_of(LATE, core, c_ref, s_ref, w_ref.at[1])
    wait(shared)
    p_ref[2] = polar_of(EARLY, 1 - core, c_ref, s_ref, w_ref.at[0])
    wait(shared_own)
    wait(shared_b)
    for copy in started:
        copy.wait_send()


def compute_kernel(c_ref, s_ref, k_ref, p_ref, q_ref, o_hbm, w_ref, l_ref, o_ref, sem):
    last = polar_of(LATE, 1 - here()[3], c_ref, s_ref, w_ref)
    for y_hi in range(2):
        for group in range(3):
            l_ref[y_hi, :, pl.ds(group * 128, 128)] = p_ref[group, :, pl.ds(y_hi * 128, 128)]
        l_ref[y_hi, :, pl.ds(384, 128)] = last[:, y_hi * 128 : y_hi * 128 + 128]
    copies = []
    for step in range(4):
        y_hi, part = divmod(step, 2)
        polar = [
            jnp.dot(l_ref[y_hi, pl.ds(h * 256, 256)], q_ref[part], preferred_element_type=jnp.float32) for h in range(2)
        ]
        for rt in range(8):
            for lt in range(2):
                parts = [
                    polar[j // 4][j % 4 * 64 + rt * 8 : j % 4 * 64 + rt * 8 + 8, lt * 128 : lt * 128 + 128] for j in range(8)
                ]
                for k in range(8):
                    total = k_ref[k * 8] * parts[0]
                    for j in range(1, 8):
                        total = total + k_ref[k * 8 + j] * parts[j]
                    o_ref[step, k, pl.ds(rt * 8, 8), pl.ds(lt * 128, 128)] = total
        copy = pltpu.make_async_copy(o_ref.at[step], o_hbm.at[:, :, pl.ds(step * 256, 256)], sem.at[step])
        copy.start()
        copies.append(copy)
    for copy in copies:
        copy.wait()


def body(row_orbitals, column_orbitals, occupation, order, levels, times, quad_weights, freqs):
    hbm = pl.BlockSpec(memory_space=pltpu.HBM)
    vmem = pl.BlockSpec(memory_space=pltpu.VMEM)
    dma = pltpu.SemaphoreType.DMA
    count = order.shape[0]
    columns, scaled, cosines, polar, order_back = pl.pallas_call(
        gather_kernel,
        out_shape=(
            pltpu.VMEM((4 * HALF, 16, 128), jnp.bfloat16),
            pltpu.VMEM((1024, 2048), jnp.bfloat16),
            pltpu.VMEM((64, 8, 128), jnp.float32),
            pltpu.VMEM((3, 512, 256), jnp.bfloat16),
            pltpu.VMEM((2, 512, 256), jnp.bfloat16),
        ),
        in_specs=[hbm] * 8,
        out_specs=(vmem,) * 5,
        scratch_shapes=[
            pltpu.VMEM((2, 256, 2048), jnp.bfloat16),
            pltpu.VMEM((8, 64, 256), jnp.bfloat16),
            pltpu.VMEM((1, count), jnp.int32),
            pltpu.VMEM((1, count), jnp.int32),
            pltpu.VMEM((count // 128, 128), jnp.float32),
            pltpu.VMEM((2, 8, count), jnp.float32),
            pltpu.SMEM((8,), jnp.float32),
            pltpu.SMEM((8,), jnp.float32),
            pltpu.SMEM((8,), jnp.float32),
            dma((2, 11)), dma((2, 11)), dma((7,)), dma((7,)), dma((3, 2, 3)), dma((3, 2, 3)), dma((3, 2, 3)), dma((3, 2, 3)),
            dma((4, 2)), dma((4, 2)), dma((10, 2)), dma((10, 2)), dma((9,)),
        ],
        compiler_params=pltpu.CompilerParams(collective_id=0, has_side_effects=True, vmem_limit_bytes=67043328 - 9961472 - 8192),
        name="gather",
    )(
        row_orbitals, column_orbitals, occupation.reshape(1, count), order.reshape(1, count),
        levels.reshape(count // 128, 128), times, quad_weights, freqs,
    )
    return pl.pallas_call(
        compute_kernel,
        out_shape=jax.ShapeDtypeStruct((8, 64, 1024), jnp.float32),
        in_specs=[vmem] * 5,
        out_specs=hbm,
        scratch_shapes=[
            pltpu.VMEM((256, 2048), jnp.bfloat16),
            pltpu.VMEM((2, 512, 512), jnp.bfloat16),
            pltpu.VMEM((4, 8, 64, 256), jnp.float32),
            dma((4,)),
        ],
        compiler_params=pltpu.CompilerParams(vmem_limit_bytes=40 * 2**20),
        name="compute",
    )(columns, scaled, cosines, polar, order_back)


def solution(mesh):
    placed = (P("space", "tm"), P("space", "tm"), P(), P(), P(), P(), P(), P())
    return jax.shard_map(
        body, mesh=mesh, in_specs=placed, out_specs=P(None, ("space", "tm"), None), check_vma=False
    )
```
